256 devices in a mesh: seq: 128 (over y, x, z), dp: 2 (over core).
Axes of the slice: x: 4, y: 4, z: 8, core: 2. Of those that a mesh axis runs over, the one named last changes fastest.
Arguments:
- tokens: bfloat16 [32768, 4096], P(('dp', 'seq')), parts along dimension 0, may hold values from -6 to 6
- sign_in: int32 [32768, 256], P(('dp', 'seq')), parts along dimension 0, may hold values from 0 to 65535
- sign_out: int32 [32768, 32], P(('dp', 'seq')), parts along dimension 0, may hold values from 0 to 65535
- w_value: bfloat16 [4096, 512], P('seq'), may hold values from -0.09375 to 0.09375
- w_noise: bfloat16 [4096, 512], P('seq'), may hold values from -0.046875 to 0.046875
- w_gate: bfloat16 [4096, 512], replicated, may hold values from -0.09375 to 0.09375
- conv_taps: float32 [3, 1024], replicated, may hold values from -3.5 to 3.5
- long_filter: float32 [16384, 512], P('seq'), may hold values from -1.5 to 1.5, as said below
- w_out: bfloat16 [512, 4096], replicated, may hold values from -0.25 to 0.25
Outputs:
- mixed: bfloat16 [32768, 4096], P(('dp', 'seq')), parts along dimension 0
The draws below stay inside these ranges and needn't reach their ends.
There are 2 independent parts, one for each index of `dp`. The reference program is written for one: setup_inputs(seed, part) draws one part's arguments, and reference() takes and returns one part's arrays. A program takes and returns all parts, laid end to end along the dimension named above; an argument that names none is the same for every part. Nothing has to cross between parts.
Inputs may be any that keep to these rules, and one draw needn't show every extreme that they name: `long_filter`: filter taps are real and finite.
All inputs are finite; a program needn't handle non-finite values.
Results may differ from the reference program's by a relative error of at most 0.0064.
Values may be sent and summed in bfloat16 or wider, within the bound.
A program may use at most 64 MiB of HBM per device.

```python
import jax
import jax.numpy as jnp
from jax import lax

D = 4096
CH = 512
TAPS = 3
SEQ = 16384


def draw_long_filter(key, part):
    rough_part = jnp.clip(jax.random.normal(key, (SEQ, CH), jnp.float32), -5.0, 5.0)
    lag_index = jnp.arange(SEQ, dtype=jnp.float32)[:, None]
    return 0.3 * rough_part * lax.rsqrt(1.0 + lag_index)


def plant(values, rng, smallest, largest):
    place = [jax.random.randint(jax.random.fold_in(rng, axis), (), 0, length) for axis, length in enumerate(values.shape)]
    main_axis = values.shape.index(max(values.shape))
    beside = place[:main_axis] + [(place[main_axis] + 1) % values.shape[main_axis]] + place[main_axis + 1:]
    return values.at[tuple(place)].set(smallest).at[tuple(beside)].set(largest)


def block_levels(own_key, dims, split, smallest, largest):
    gain, own = 1.0, jax.random.fold_in(own_key, 6)
    for axis_at, blocks in split:
        heights = jnp.exp(jax.random.uniform(jax.random.fold_in(own, axis_at), (blocks,), jnp.float32, smallest / len(split), largest / len(split)))
        gain = gain * jnp.repeat(heights, dims[axis_at] // blocks).reshape([-1 if axis == axis_at else 1 for axis in range(len(dims))])
    return gain


def noise(stream_key, shape, width, reach, pieces=(), kind=jnp.bfloat16):
    result = jax.random.normal(stream_key, shape, jnp.float32) * width
    if len(pieces) > 0:
        result = block_levels(stream_key, shape, pieces, -0.22, 0.18) * result
    return jnp.clip(result, min=-reach, max=reach).astype(kind)


def setup_inputs(seed: int = 0, part: int = 0) -> dict:
    key_of = jax.random.split(jax.random.key(seed), 10)
    part_splits = jax.random.split(jax.random.fold_in(key_of[9], part), 10)
    return {
        "tokens": noise(part_splits[0], (SEQ, D), 1.0, 6.0, ((0, 128),)),
        "sign_in": plant(jax.random.randint(part_splits[1], (SEQ, D // 16), 0, 65536), jax.random.fold_in(part_splits[1], 1), 0, 65535).astype(jnp.int32),
        "sign_out": plant(jax.random.randint(part_splits[2], (SEQ, CH // 16), 0, 65536), jax.random.fold_in(part_splits[2], 1), 0, 65535).astype(jnp.int32),
        "w_value": noise(key_of[3], (D, CH), D ** -0.5, 0.09375, ((0, 128),)),
        "w_noise": noise(key_of[4], (D, CH), (4 * D) ** -0.5, 0.046875, ((0, 128),)),
        "w_gate": noise(key_of[5], (D, CH), D ** -0.5, 0.09375),
        "conv_taps": noise(key_of[6], (TAPS, 2 * CH), TAPS ** -0.5, 3.5, (), jnp.float32),
        "long_filter": draw_long_filter(jax.random.fold_in(key_of[9], 71), part),
        "w_out": noise(key_of[8], (CH, D), CH ** -0.5, 0.25),
    }


HIGHEST = lax.Precision.HIGHEST


def unpack_signs(packed):
    shifts = jnp.arange(16, dtype=jnp.int32)
    bit_table = jnp.bitwise_and(jnp.right_shift(packed[:, :, None], shifts[None, None, :]), 1)
    return (2 * bit_table - 1).reshape(packed.shape[0], packed.shape[1] * 16)


def reference(tokens, sign_in, sign_out, w_value, w_noise, w_gate, conv_taps, long_filter, w_out):
    flip_in = unpack_signs(sign_in).astype(jnp.bfloat16)
    flip_out = unpack_signs(sign_out).astype(jnp.float32)
    mean_part = jnp.dot(tokens, w_value, preferred_element_type=jnp.float32)
    noise_part = jnp.dot(tokens * flip_in, w_noise, preferred_element_type=jnp.float32)
    value_rows = (mean_part + flip_out * noise_part).astype(jnp.bfloat16)
    gate_rows = jnp.dot(tokens, w_gate, preferred_element_type=jnp.float32).astype(jnp.bfloat16)
    streams = jnp.concatenate([value_rows, gate_rows], axis=1).astype(jnp.float32)
    padded = jnp.concatenate([jnp.zeros((TAPS - 1, streams.shape[1]), jnp.float32), streams], axis=0)
    kernel = conv_taps[::-1][:, None, :]
    filtered = lax.conv_general_dilated(padded[None], kernel, (1,), "VALID", dimension_numbers=("NWC", "WIO", "NWC"), feature_group_count=streams.shape[1], precision=HIGHEST)[0]
    signal = filtered[:, :CH]
    gate_short = filtered[:, CH:]
    spec_signal = jnp.fft.fft(jnp.concatenate([signal, jnp.zeros_like(signal)], axis=0), axis=0)
    spec_filter = jnp.fft.fft(jnp.concatenate([long_filter, jnp.zeros_like(long_filter)], axis=0), axis=0)
    long_mixed = jnp.real(jnp.fft.ifft(spec_signal * spec_filter, axis=0))[:SEQ].astype(jnp.float32)
    gated_mix = (gate_short * long_mixed).astype(jnp.bfloat16)
    return jnp.dot(gated_mix, w_out, preferred_element_type=jnp.float32).astype(jnp.bfloat16)
```

```python
import functools

import jax
import jax.numpy as jnp
from jax import lax
from jax.experimental import pallas as pl
from jax.experimental.pallas import tpu as pltpu
from jax.sharding import PartitionSpec as P

MESH = pl.DeviceIdType.MESH
NY, NX, NZ = 4, 4, 8
NS = NY * NX * NZ
SIZE = {"x": NX, "y": NY, "z": NZ}
D, CH, TOK, HALF = 4096, 512, 128, 256
F32, BF16 = jnp.float32, jnp.bfloat16
ROWS = (32, 48, 48)
ORDERS = ("xyz", "zyx", "zxy")


def unpack_signs(packed):
    shifts = jnp.arange(16, dtype=jnp.int32)
    bit_table = jnp.bitwise_and(jnp.right_shift(packed[:, :, None], shifts[None, None, :]), 1)
    return (2 * bit_table - 1).reshape(packed.shape[0], packed.shape[1] * 16)


def body(
    tok_ref, flp_ref, fo_ref, wv_ref, wn_ref, wg_ref, taps_ref, gtaps_ref, filt_ref,
    gm_ref,
    wa, wb, wc, tokall, flpall, foall, wg, gpad, halo, fsend, frecv, gcomp, tmat,
    vacc, nacc, vsend, vrecv, xpad, xx, yacc, ysend, yrecv, gmsend,
    ag_send, ag_recv, sib_send, sib_recv, loc_sem, bar_y, bar_z,
    f_send, f_recv, h_send, h_recv, v_send, v_recv, y_send, y_recv,
):
    s = lax.axis_index("seq")
    dp = lax.axis_index("dp")
    pos = {"z": lax.rem(s, NZ), "x": lax.rem(s // NZ, NX), "y": s // (NZ * NX)}

    def at(axis, step):
        p = dict(pos)
        p[axis] = ring(axis, step)
        return {"seq": (p["y"] * NX + p["x"]) * NZ + p["z"], "dp": dp}

    def ring(axis, step):
        return lax.rem(pos[axis] + step + SIZE[axis], SIZE[axis])

    sibling = {"seq": s, "dp": 1 - dp}

    cols = pl.ds(pl.multiple_of(dp * HALF, HALF), HALF)
    cols_other = pl.ds(pl.multiple_of((1 - dp) * HALF, HALF), HALF)
    local = [
        pltpu.make_async_copy(wg_ref.at[:, cols], wg, loc_sem.at[0]),
        pltpu.make_async_copy(tok_ref, tokall.at[pl.ds(0, TOK)], loc_sem.at[1]),
        pltpu.make_async_copy(flp_ref, flpall.at[pl.ds(0, TOK)], loc_sem.at[2]),
        pltpu.make_async_copy(fo_ref.at[:, cols], foall.at[pl.ds(0, TOK)], loc_sem.at[3]),
    ]
    for c in local:
        c.start()

    bar = pltpu.get_barrier_semaphore()
    for axis in "xyz":
        for step in range(1, SIZE[axis]):
            pl.semaphore_signal(bar, inc=1, device_id=at(axis, step), device_id_type=MESH)
    pl.semaphore_signal(bar, inc=1, device_id=sibling, device_id_type=MESH)

    here = (pos["y"], pos["x"], pos["z"])
    wv, wn = wv_ref[:, cols], wn_ref[:, cols]
    wa[here] = wv[:, :128]
    wb[here] = jnp.concatenate([wn[:, :128], wv[:16, 128:]], axis=0)
    wc[here] = jnp.concatenate([wv[16:, 128:], wn[:, 128:]], axis=0)
    pl.semaphore_wait(bar, 14)

    used = [0]
    sent = []

    def remote(ref, dev):
        i = used[0]
        used[0] += 1
        c = pltpu.make_async_remote_copy(
            src_ref=ref, dst_ref=ref, send_sem=ag_send.at[i], recv_sem=ag_recv.at[i],
            device_id=dev, device_id_type=MESH,
        )
        c.start()
        sent.append(c)
        return c

    def gather(w, order):
        have = []

        def unit(axis, p, half=None):
            idx = {a: (slice(None) if a in have else pos[a]) for a in "yxz"}
            idx[axis] = p
            if half is not None:
                n = SIZE[have[-1]] // 2
                idx[have[-1]] = pl.ds(half * n, n)
            return w.at[idx["y"], idx["x"], idx["z"]]

        a = order[0]
        flight = [remote(unit(a, pos[a]), at(a, k)) for k in range(1, SIZE[a])]
        yield
        for c in flight:
            c.wait_recv()
        have.append(a)
        for a in order[1:]:
            for step in range(1, SIZE[a] // 2 + 1):
                last = step == SIZE[a] // 2
                up = remote(unit(a, ring(a, 1 - step), 0 if last else None), at(a, 1))
                down = remote(unit(a, ring(a, step - 1), 1 if last else None), at(a, -1))
                yield
                up.wait_recv()
                down.wait_recv()
            have.append(a)

    def to_all(src, dst, send_sem, recv_sem, first, last):
        def send(i, _):
            peer = lax.rem(s + i, NS)
            pltpu.make_async_remote_copy(
                src_ref=src.at[peer], dst_ref=dst.at[s], send_sem=send_sem, recv_sem=recv_sem,
                device_id={"seq": peer, "dp": dp}, device_id_type=MESH,
            ).start()
            return 0

        lax.fori_loop(first, last, send, 0)

    def all_landed(src, dst, send_sem, recv_sem):
        c = pltpu.make_async_remote_copy(
            src_ref=src.at[pl.ds(0, NS - 1)], dst_ref=dst.at[pl.ds(0, NS - 1)],
            send_sem=send_sem, recv_sem=recv_sem,
            device_id=sibling, device_id_type=MESH,
        )
        c.wait_send()
        c.wait_recv()

    exchange = [
        pltpu.make_async_remote_copy(
            src_ref=src, dst_ref=dst, send_sem=sib_send.at[i], recv_sem=sib_recv.at[i],
            device_id=sibling, device_id_type=MESH,
        )
        for i, (src, dst) in enumerate([
            (tok_ref, tokall.at[pl.ds(TOK, TOK)]),
            (flp_ref, flpall.at[pl.ds(TOK, TOK)]),
            (fo_ref.at[:, cols_other], foall.at[pl.ds(TOK, TOK)]),
        ])
    ]

    def filter_out():
        for c in exchange:
            c.start()
        for step in range(1, NY):
            pl.semaphore_signal(bar_y, inc=1, device_id=at("y", step), device_id_type=MESH)
        mine = filt_ref[:, cols]
        for c in range(2):
            fsend[:, c, :] = mine[:, 128 * c : 128 * c + 128].T
        pl.semaphore_wait(bar_y, NY - 1)
        for step in range(1, NZ):
            pl.semaphore_signal(bar_z, inc=1, device_id=at("z", step), device_id_type=MESH)

    def send_filter(first, last):
        if first == 1:
            pl.semaphore_wait(bar_z, NZ - 1)
            frecv[s] = fsend[s]
        to_all(fsend, frecv, f_send, f_recv, first, last)

    halo_copy = pltpu.make_async_remote_copy(
        src_ref=gpad.at[:, pl.ds(TOK, 8)], dst_ref=halo, send_sem=h_send, recv_sem=h_recv,
        device_id={"seq": lax.rem(s + 1, NS), "dp": dp}, device_id_type=MESH,
    )

    def gate():
        local[0].wait()
        local[1].wait()
        exchange[0].wait()
        rows = jnp.dot(tokall[...], wg[...], preferred_element_type=F32).astype(BF16).astype(F32)
        gpad[0, pl.ds(8, TOK)] = rows[:TOK]
        gpad[1, pl.ds(8, TOK)] = rows[TOK:]
        halo_copy.start()

    lane = lax.broadcasted_iota(jnp.int32, (128, 128), 1)
    row = lax.broadcasted_iota(jnp.int32, (128, 128), 0)

    def compose():
        all_landed(fsend, frecv, f_send, f_recv)
        for c in range(2):
            h = frecv[:, c, :]
            chan = dp * HALF + c * 128 + s
            total = taps_ref[0, chan] * h
            for j in (1, 2):
                turned = pltpu.roll(h, j, 1)
                before = jnp.where(row == 0, 0.0, pltpu.roll(turned, 1, 0))
                total = total + taps_ref[j, chan] * jnp.where(lane < j, before, turned)
            gcomp[c] = total

    def toeplitz(c):
        def step(k, past):
            line = jnp.broadcast_to(gcomp[c, pl.ds(k, 1), :], (128, 128))
            turned = pltpu.roll(line, 0, 1, stride=1, stride_axis=0)
            tmat[c, pl.ds(pl.multiple_of(k * 128, 128), 128), :] = jnp.where(
                lane >= row, turned, past
            ).astype(BF16)
            return turned

        lax.fori_loop(0, NS, step, jnp.zeros((128, 128), F32))

    tasks = [
        filter_out,
        lambda: send_filter(1, 64),
        lambda: send_filter(64, NS),
        gate,
        lambda: (compose(), toeplitz(0)),
        lambda: toeplitz(1),
    ]
    running = [gather(w, order) for w, order in zip((wa, wb, wc), ORDERS)]
    while running:
        for g in list(running):
            try:
                next(g)
            except StopIteration:
                running.remove(g)
        if tasks:
            tasks.pop(0)()
    for task in tasks:
        task()

    for c in (local[2], local[3]):
        c.wait()
    for c in exchange[1:]:
        c.wait()
    vacc[...] = jnp.zeros_like(vacc)
    nacc[...] = jnp.zeros_like(nacc)

    def project(i, _):
        y, x = i // NX, lax.rem(i, NX)
        k = pl.ds(pl.multiple_of(i * 256, 256), 256)
        pa, pb, pc = wa[y, x], wb[y, x], wc[y, x]
        right = jnp.concatenate([pb[:, 32:], pc[:, :16]], axis=1).reshape(256, 128)
        value = jnp.concatenate([pa.reshape(256, 128), right], axis=1)
        noise = jnp.concatenate(
            [pb[:, :32].reshape(256, 128), pc[:, 16:].reshape(256, 128)], axis=1
        )
        vacc[...] += jnp.dot(tokall[:, k], value, preferred_element_type=F32)
        nacc[...] += jnp.dot(flpall[:, k], noise, preferred_element_type=F32)
        return 0

    lax.fori_loop(0, NY * NX, project, 0)
    value_rows = (vacc[...] + foall[...] * nacc[...]).astype(BF16).astype(F32)
    for p in range(2):
        for c in range(2):
            vsend[:, 2 * p + c, :] = value_rows[128 * p : 128 * p + 128, 128 * c : 128 * c + 128].T
    vrecv[s] = vsend[s]
    to_all(vsend, vrecv, v_send, v_recv, 1, NS)
    all_landed(vsend, vrecv, v_send, v_recv)

    xpad[:, pl.ds(0, 16), :] = jnp.zeros((4, 16, 128), F32)
    for p in range(2):
        for c in range(2):
            xpad[2 * p + c, pl.ds(16, 128), :] = vrecv[:, 2 * p + c, :]
    for p in range(2):
        for c in range(2):
            for r in range(16):
                late = xpad[2 * p + c, pl.ds(16 - r, 128), :].astype(BF16)
                xx[c, r // 2, :, p, :, pl.ds(128 * (r % 2), 128)] = late.reshape(8, 16, 128)
    for c in range(2):
        for u in range(8):
            m = 8 - u
            total = None
            for k in range(8):
                part = jnp.dot(
                    xx[c, k, pl.ds(0, m)].reshape(32 * m, 256),
                    tmat[c, pl.ds(256 * (8 * u + k), 256), :],
                    preferred_element_type=F32,
                )
                total = part if total is None else total + part
            total = total.reshape(m, 2, 16, 128)
            if u == 0:
                yacc[c] = total
            else:
                yacc[c, pl.ds(u, m)] += total
        for p in range(2):
            ysend[:, 2 * p + c, :] = yacc[c, :, p].reshape(128, 128)
    yrecv[s] = ysend[s]
    to_all(ysend, yrecv, y_send, y_recv, 1, NS)

    halo_copy.wait()
    for p in range(2):
        gpad[p, pl.ds(0, 8)] = jnp.where(s == 0, 0.0, halo[p])
    all_landed(ysend, yrecv, y_send, y_recv)
    taps = gtaps_ref[:, cols]

    def mixed(p):
        short = taps[0:1] * gpad[p, pl.ds(8, TOK)]
        for j in (1, 2):
            short = short + taps[j : j + 1] * gpad[p, pl.ds(8 - j, TOK)]
        spread = jnp.concatenate([yrecv[:, 2 * p + c, :].T for c in range(2)], axis=1)
        return (short * spread).astype(BF16)

    gmsend[...] = mixed(1)
    swap = pltpu.make_async_remote_copy(
        src_ref=gmsend, dst_ref=gm_ref.at[:, cols], send_sem=sib_send.at[3],
        recv_sem=sib_recv.at[3], device_id=sibling, device_id_type=MESH,
    )
    swap.start()
    gm_ref[:, cols] = mixed(0)
    swap.wait()
    for c in sent:
        c.wait_send()


def on_device(tokens, sign_in, sign_out, w_value, w_noise, w_gate, conv_taps, long_filter, w_out):
    flipped = tokens * unpack_signs(sign_in).astype(BF16)
    flip_out = unpack_signs(sign_out).astype(F32)
    vmem = pl.BlockSpec(memory_space=pltpu.VMEM)
    hbm = pl.BlockSpec(memory_space=pl.ANY)
    dma, regular = pltpu.SemaphoreType.DMA, pltpu.SemaphoreType.REGULAR
    exchange = [pltpu.VMEM((NS, 4, 128), F32)]
    gated = pl.pallas_call(
        body,
        out_shape=jax.ShapeDtypeStruct((TOK, CH), BF16),
        in_specs=[
            hbm, hbm, hbm, vmem, vmem, hbm, pl.BlockSpec(memory_space=pltpu.SMEM), vmem, vmem,
        ],
        out_specs=vmem,
        scratch_shapes=[pltpu.VMEM((NY, NX, NZ, r, 128), BF16) for r in ROWS]
        + [
            pltpu.VMEM((2 * TOK, D), BF16),
            pltpu.VMEM((2 * TOK, D), BF16),
            pltpu.VMEM((2 * TOK, HALF), F32),
            pltpu.VMEM((D, HALF), BF16),
            pltpu.VMEM((2, 8 + TOK, HALF), F32),
            pltpu.VMEM((2, 8, HALF), F32),
            pltpu.VMEM((NS, 2, 128), F32),
            pltpu.VMEM((NS, 2, 128), F32),
            pltpu.VMEM((2, 128, 128), F32),
            pltpu.VMEM((2, NS * TOK, 128), BF16),
            pltpu.VMEM((2 * TOK, HALF), F32),
            pltpu.VMEM((2 * TOK, HALF), F32),
        ]
        + exchange * 2
        + [
            pltpu.VMEM((4, 16 + TOK, 128), F32),
            pltpu.VMEM((2, 8, 8, 2, 16, 256), BF16),
            pltpu.VMEM((2, 8, 2, 16, 128), F32),
        ]
        + exchange * 2
        + [
            pltpu.VMEM((TOK, HALF), BF16),
            dma((64,)), dma((64,)), dma((4,)), dma((4,)), dma((4,)), regular, regular,
        ]
        + [dma] * 8,
        compiler_params=pltpu.CompilerParams(
            collective_id=0, has_side_effects=True, vmem_limit_bytes=56 << 20
        ),
    )(
        tokens, flipped, flip_out, w_value, w_noise, w_gate, conv_taps, conv_taps[:, CH:],
        long_filter,
    )
    return jnp.dot(gated, w_out, preferred_element_type=F32).astype(BF16)


def solution(mesh):
    placed = (
        P(("dp", "seq"), None),
        P(("dp", "seq"), None),
        P(("dp", "seq"), None),
        P("seq", None),
        P("seq", None),
        P(),
        P(),
        P("seq", None),
        P(),
    )
    return jax.shard_map(
        on_device, mesh=mesh, in_specs=placed, out_specs=P(("dp", "seq"), None), check_vma=False
    )
```

```python
import functools

import jax
import jax.numpy as jnp
from jax import lax
from jax.experimental import pallas as pl
from jax.experimental.pallas import tpu as pltpu
from jax.sharding import PartitionSpec as P

MESH = pl.DeviceIdType.MESH
NY, NX, NZ = 4, 4, 8
NS = NY * NX * NZ
SIZE = {"x": NX, "y": NY, "z": NZ}
D, CH, TOK, HALF = 4096, 512, 128, 256
F32, BF16 = jnp.float32, jnp.bfloat16
ROWS = (32, 48, 48)
ORDERS = ("xyz", "zyx", "zxy")


def body(
    tok_ref, sin_ref, sout_ref, wv_ref, wn_ref, wg_ref, taps_ref, gtaps_ref, filt_ref,
    gm_ref,
    wa, wb, wc, tokall, flpall, foall, wg, gpad, halo, fsend, frecv, gcomp, tmat,
    vacc, nacc, stage, vsend, vrecv, xpad, xx, yacc, ysend, yrecv, gmsend,
    sin, sout, fout, wv, wn, filt, gtaps, spread, lagged, shifts,
    ag_send, ag_recv, sib_send, sib_recv, loc_sem, bar_y, bar_z,
    f_send, f_recv, h_send, h_recv, v_send, v_recv, y_send, y_recv,
):
    s = lax.axis_index("seq")
    dp = lax.axis_index("dp")
    pos = {"z": lax.rem(s, NZ), "x": lax.rem(s // NZ, NX), "y": s // (NZ * NX)}

    def at(axis, step):
        p = dict(pos)
        p[axis] = ring(axis, step)
        return {"seq": (p["y"] * NX + p["x"]) * NZ + p["z"], "dp": dp}

    def ring(axis, step):
        return lax.rem(pos[axis] + step + SIZE[axis], SIZE[axis])

    sibling = {"seq": s, "dp": 1 - dp}

    cols = pl.ds(pl.multiple_of(dp * HALF, HALF), HALF)
    cols_other = pl.ds(pl.multiple_of((1 - dp) * HALF, HALF), HALF)
    local = [
        pltpu.make_async_copy(wg_ref.at[:, cols], wg, loc_sem.at[0]),
        pltpu.make_async_copy(tok_ref, tokall.at[pl.ds(0, TOK)], loc_sem.at[1]),
        pltpu.make_async_copy(wv_ref.at[:, cols], wv, loc_sem.at[2]),
        pltpu.make_async_copy(wn_ref.at[:, cols], wn, loc_sem.at[3]),
        pltpu.make_async_copy(filt_ref.at[:, cols], filt, loc_sem.at[4]),
        pltpu.make_async_copy(sin_ref, sin, loc_sem.at[5]),
        pltpu.make_async_copy(gtaps_ref.at[:, pl.ds(CH, CH)], gtaps, loc_sem.at[6]),
    ]
    for i in (2, 3, 4, 1, 5, 0, 6):
        local[i].start()

    bar = pltpu.get_barrier_semaphore()
    for axis in "xyz":
        for step in range(1, SIZE[axis]):
            pl.semaphore_signal(bar, inc=1, device_id=at(axis, step), device_id_type=MESH)
    pl.semaphore_signal(bar, inc=1, device_id=sibling, device_id_type=MESH)

    here = (pos["y"], pos["x"], pos["z"])
    local[2].wait()
    local[3].wait()
    wa[here] = wv[:, :128]
    wb[here] = jnp.concatenate([wn[:, :128], wv[:16, 128:]], axis=0)
    wc[here] = jnp.concatenate([wv[16:, 128:], wn[:, 128:]], axis=0)
    pl.semaphore_wait(bar, 14)

    used = [0]
    sent = []

    def remote(ref, dev):
        i = used[0]
        used[0] += 1
        c = pltpu.make_async_remote_copy(
            src_ref=ref, dst_ref=ref, send_sem=ag_send.at[i], recv_sem=ag_recv.at[i],
            device_id=dev, device_id_type=MESH,
        )
        c.start()
        sent.append(c)
        return c

    def gather(w, order, rows):
        have = []

        def unit(axis, p, half=None):
            idx = {a: (slice(None) if a in have else pos[a]) for a in "yxz"}
            idx[axis] = p
            if half is not None:
                n = SIZE[have[-1]] // 2
                idx[have[-1]] = pl.ds(half * n, n)
            return w.at[idx["y"], idx["x"], idx["z"], rows]

        a = order[0]
        flight = [remote(unit(a, pos[a]), at(a, k)) for k in range(1, SIZE[a])]
        yield
        for c in flight:
            c.wait_recv()
        have.append(a)
        for a in order[1:]:
            for step in range(1, SIZE[a] // 2 + 1):
                last = step == SIZE[a] // 2
                up = remote(unit(a, ring(a, 1 - step), 0 if last else None), at(a, 1))
                down = remote(unit(a, ring(a, step - 1), 1 if last else None), at(a, -1))
                yield
                up.wait_recv()
                down.wait_recv()
            have.append(a)

    def to_all(src, dst, send_sem, recv_sem, first, last):
        def send(i, _):
            peer = lax.rem(s + i, NS)
            pltpu.make_async_remote_copy(
                src_ref=src.at[peer], dst_ref=dst.at[s], send_sem=send_sem, recv_sem=recv_sem,
                device_id={"seq": peer, "dp": dp}, device_id_type=MESH,
            ).start()
            return 0

        lax.fori_loop(first, last, send, 0)

    def all_landed(src, dst, send_sem, recv_sem):
        c = pltpu.make_async_remote_copy(
            src_ref=src.at[pl.ds(0, NS - 1)], dst_ref=dst.at[pl.ds(0, NS - 1)],
            send_sem=send_sem, recv_sem=recv_sem,
            device_id=sibling, device_id_type=MESH,
        )
        c.wait_send()
        c.wait_recv()

    exchange = [
        pltpu.make_async_remote_copy(
            src_ref=src, dst_ref=dst, send_sem=sib_send.at[i], recv_sem=sib_recv.at[i],
            device_id=sibling, device_id_type=MESH,
        )
        for i, (src, dst) in enumerate([
            (tok_ref, tokall.at[pl.ds(TOK, TOK)]),
            (flpall.at[pl.ds(0, TOK)], flpall.at[pl.ds(TOK, TOK)]),
            (fout.at[:, cols_other], foall.at[pl.ds(TOK, TOK)]),
        ])
    ]

    def filter_out():
        exchange[0].start()
        for step in range(1, NY):
            pl.semaphore_signal(bar_y, inc=1, device_id=at("y", step), device_id_type=MESH)
        local[4].wait()
        for c in range(2):
            fsend[:, c, :] = filt[:, pl.ds(128 * c, 128)].T
        pl.semaphore_wait(bar_y, NY - 1)
        for step in range(1, NZ):
            pl.semaphore_signal(bar_z, inc=1, device_id=at("z", step), device_id_type=MESH)

    def send_filter(first, last):
        if first == 1:
            pl.semaphore_wait(bar_z, NZ - 1)
            frecv[s] = fsend[s]
        to_all(fsend, frecv, f_send, f_recv, first, last)

    halo_copy = pltpu.make_async_remote_copy(
        src_ref=gpad.at[:, pl.ds(TOK, 8)], dst_ref=halo, send_sem=h_send, recv_sem=h_recv,
        device_id={"seq": lax.rem(s + 1, NS), "dp": dp}, device_id_type=MESH,
    )

    def gate():
        local[0].wait()
        exchange[0].wait()
        rows = jnp.dot(tokall[...], wg[...], preferred_element_type=F32).astype(BF16).astype(F32)
        gpad[0, pl.ds(8, TOK)] = rows[:TOK]
        gpad[1, pl.ds(8, TOK)] = rows[TOK:]
        halo_copy.start()

    def bit_table():
        word = lax.broadcasted_iota(jnp.int32, (256, 256), 0)
        place = lax.broadcasted_iota(jnp.int32, (256, 256), 1)
        target = place // 16 + 128 * (lax.rem(place, 16) // 8)
        for i in range(8):
            spread[:, pl.ds(256 * i, 256)] = (word == target + 16 * i).astype(F32).astype(BF16)

    def signs(words, count):
        halves = jnp.concatenate([words & 255, words >> 8], axis=1).astype(F32).astype(BF16)
        found = jnp.dot(halves, spread[:, pl.ds(0, count)], preferred_element_type=F32)
        bit = lax.rem(lax.broadcasted_iota(jnp.int32, (TOK, count), 1), 8)
        return (2 * ((found.astype(jnp.int32) >> bit) & 1) - 1).astype(F32)

    def flip():
        bit_table()
        sout[...] = jnp.zeros_like(sout)
        sout[:, pl.ds(0, 32)] = sout_ref[...]
        for i in (1, 5):
            local[i].wait()
        for i in range(2):
            at_i = pl.ds(2048 * i, 2048)
            turned = signs(sin[:, pl.ds(128 * i, 128)], 2048)
            flpall[pl.ds(0, TOK), at_i] = (tokall[pl.ds(0, TOK), at_i].astype(F32) * turned).astype(BF16)
        fout[...] = signs(sout[...], CH)
        exchange[1].start()
        exchange[2].start()
        foall[pl.ds(0, TOK)] = fout[:, cols]

    lane = lax.broadcasted_iota(jnp.int32, (128, 128), 1)
    row = lax.broadcasted_iota(jnp.int32, (128, 128), 0)

    def compose():
        all_landed(fsend, frecv, f_send, f_recv)
        for c in range(2):
            h = frecv[:, c, :]
            chan = dp * HALF + c * 128 + s
            total = taps_ref[0, chan] * h
            for j in (1, 2):
                turned = pltpu.roll(h, j, 1)
                before = jnp.where(row == 0, 0.0, pltpu.roll(turned, 1, 0))
                total = total + taps_ref[j, chan] * jnp.where(lane < j, before, turned)
            gcomp[c] = total

    def shift_table():
        source = lax.broadcasted_iota(jnp.int32, (256, 128), 0)
        target = lax.broadcasted_iota(jnp.int32, (256, 128), 1) + 128
        for r in range(8):
            shifts[:, pl.ds(128 * r, 128)] = (source == target - 16 * r).astype(F32).astype(BF16)
        lagged[:, 0] = jnp.zeros((2, 16, 128), BF16)

    low_lane = lax.broadcasted_iota(jnp.int32, (16, 128), 1)
    low_row = lax.broadcasted_iota(jnp.int32, (16, 128), 0)

    def toeplitz(c):
        def lags(i, past):
            for k in range(8):
                line = jnp.broadcast_to(gcomp[c, pl.ds(8 * i + k, 1), :], (16, 128))
                turned = pltpu.roll(line, 0, 1, stride=1, stride_axis=0)
                lagged[c, 1 + 8 * i + k] = jnp.where(low_lane >= low_row, turned, past).astype(BF16)
                past = turned
            return past

        lax.fori_loop(0, NS // 8, lags, jnp.zeros((16, 128), F32))

        def expand(i, _):
            k = pl.multiple_of(16 * i, 16)
            pair = jnp.concatenate(
                [
                    lagged[c, pl.ds(k, 16)].reshape(256, 128),
                    lagged[c, pl.ds(k + 1, 16)].reshape(256, 128),
                ],
                axis=1,
            )
            for r in range(0, 8, 2):
                out = jnp.dot(pair, shifts[:, pl.ds(128 * r, 256)], preferred_element_type=F32)
                out = out.astype(BF16)
                tmat[c, pl.ds(k, 16), r] = out[:, :128].reshape(16, 16, 128)
                tmat[c, pl.ds(k, 16), r + 1] = out[:, 128:].reshape(16, 16, 128)
            return 0

        lax.fori_loop(0, NS // 16, expand, 0)

    tasks = [
        filter_out,
        flip,
        lambda: send_filter(1, 64),
        lambda: send_filter(64, NS),
        gate,
        shift_table,
        lambda: (compose(), toeplitz(0)),
        lambda: toeplitz(1),
    ]
    cuts = (
        ((wa, 0, 16), (wb, 0, 32), (wc, 0, 16)),
        ((wa, 16, 16), (wb, 32, 16), (wc, 16, 32)),
    )
    running = [
        [gather(w, order, pl.ds(first, rows)) for (w, first, rows), order in zip(cut, ORDERS)]
        for cut in cuts
    ]
    while running:
        for group in list(running):
            for g in list(group):
                try:
                    next(g)
                except StopIteration:
                    group.remove(g)
            if not group:
                running.remove(group)
            if tasks and (len(tasks) < 8 or group is running[-1]):
                tasks.pop(0)()
    for task in tasks:
        task()

    for c in exchange[1:]:
        c.wait()
    vacc[...] = jnp.zeros_like(vacc)
    nacc[...] = jnp.zeros_like(nacc)

    def project(i, _):
        y, x = i // NX, lax.rem(i, NX)
        k = pl.ds(pl.multiple_of(i * 256, 256), 256)
        pa, pb, pc = wa[y, x], wb[y, x], wc[y, x]
        right = jnp.concatenate([pb[:, 32:], pc[:, :16]], axis=1).reshape(256, 128)
        value = jnp.concatenate([pa.reshape(256, 128), right], axis=1)
        noise = jnp.concatenate(
            [pb[:, :32].reshape(256, 128), pc[:, 16:].reshape(256, 128)], axis=1
        )
        vacc[...] += jnp.dot(tokall[:, k], value, preferred_element_type=F32)
        nacc[...] += jnp.dot(flpall[:, k], noise, preferred_element_type=F32)
        return 0

    lax.fori_loop(0, NY * NX, project, 0)
    value_rows = (vacc[...] + foall[...] * nacc[...]).astype(BF16).astype(F32)
    for p in range(2):
        for c in range(2):
            stage[:, 2 * p + c, :] = value_rows[128 * p : 128 * p + 128, 128 * c : 128 * c + 128].T
    vsend[...] = stage[...].astype(BF16)
    vrecv[s] = vsend[s]
    to_all(vsend, vrecv, v_send, v_recv, 1, NS)
    all_landed(vsend, vrecv, v_send, v_recv)

    stage[...] = vrecv[...].astype(F32)
    xpad[:, pl.ds(0, 16), :] = jnp.zeros((4, 16, 128), F32)
    for p in range(2):
        for c in range(2):
            xpad[2 * p + c, pl.ds(16, 128), :] = stage[:, 2 * p + c, :]
    for p in range(2):
        for c in range(2):
            for r in range(16):
                late = xpad[2 * p + c, pl.ds(16 - r, 128), :].astype(BF16)
                xx[c, r // 2, :, p, :, pl.ds(128 * (r % 2), 128)] = late.reshape(8, 16, 128)
    for c in range(2):
        for u in range(8):
            m = 8 - u
            total = None
            for k in range(8):
                part = jnp.dot(
                    xx[c, k, pl.ds(0, m)].reshape(32 * m, 256),
                    tmat[c, pl.ds(2 * (8 * u + k), 2)].reshape(256, 128),
                    preferred_element_type=F32,
                )
                total = part if total is None else total + part
            total = total.reshape(m, 2, 16, 128)
            if u == 0:
                yacc[c] = total
            else:
                yacc[c, pl.ds(u, m)] += total
        for p in range(2):
            stage[:, 2 * p + c, :] = yacc[c, :, p].reshape(128, 128)
    ysend[...] = stage[...].astype(BF16)
    yrecv[s] = ysend[s]
    to_all(ysend, yrecv, y_send, y_recv, 1, NS)

    halo_copy.wait()
    for p in range(2):
        gpad[p, pl.ds(0, 8)] = jnp.where(s == 0, 0.0, halo[p])
    all_landed(ysend, yrecv, y_send, y_recv)
    stage[...] = yrecv[...].astype(F32)
    local[6].wait()
    taps = gtaps[:, cols]

    def mixed(p):
        short = taps[0:1] * gpad[p, pl.ds(8, TOK)]
        for j in (1, 2):
            short = short + taps[j : j + 1] * gpad[p, pl.ds(8 - j, TOK)]
        mix = jnp.concatenate([stage[:, 2 * p + c, :].T for c in range(2)], axis=1)
        return (short * mix).astype(BF16)

    gmsend[...] = mixed(1)
    swap = pltpu.make_async_remote_copy(
        src_ref=gmsend, dst_ref=gm_ref.at[:, cols], send_sem=sib_send.at[3],
        recv_sem=sib_recv.at[3], device_id=sibling, device_id_type=MESH,
    )
    swap.start()
    gm_ref[:, cols] = mixed(0)
    swap.wait()
    for c in sent:
        c.wait_send()


def on_device(tokens, sign_in, sign_out, w_value, w_noise, w_gate, conv_taps, long_filter, w_out):
    vmem = pl.BlockSpec(memory_space=pltpu.VMEM)
    hbm = pl.BlockSpec(memory_space=pl.ANY)
    dma, regular = pltpu.SemaphoreType.DMA, pltpu.SemaphoreType.REGULAR
    exchange = [pltpu.VMEM((NS, 4, 128), BF16)]
    gated = pl.pallas_call(
        body,
        out_shape=jax.ShapeDtypeStruct((TOK, CH), BF16),
        in_specs=[
            hbm, hbm, vmem, hbm, hbm, hbm, pl.BlockSpec(memory_space=pltpu.SMEM), hbm, hbm,
        ],
        out_specs=vmem,
        scratch_shapes=[pltpu.VMEM((NY, NX, NZ, r, 128), BF16) for r in ROWS]
        + [
            pltpu.VMEM((2 * TOK, D), BF16),
            pltpu.VMEM((2 * TOK, D), BF16),
            pltpu.VMEM((2 * TOK, HALF), F32),
            pltpu.VMEM((D, HALF), BF16),
            pltpu.VMEM((2, 8 + TOK, HALF), F32),
            pltpu.VMEM((2, 8, HALF), F32),
            pltpu.VMEM((NS, 2, 128), F32),
            pltpu.VMEM((NS, 2, 128), F32),
            pltpu.VMEM((2, 128, 128), F32),
            pltpu.VMEM((2, NS, 8, 16, 128), BF16),
            pltpu.VMEM((2 * TOK, HALF), F32),
            pltpu.VMEM((2 * TOK, HALF), F32),
            pltpu.VMEM((NS, 4, 128), F32),
        ]
        + exchange * 2
        + [
            pltpu.VMEM((4, 16 + TOK, 128), F32),
            pltpu.VMEM((2, 8, 8, 2, 16, 256), BF16),
            pltpu.VMEM((2, 8, 2, 16, 128), F32),
        ]
        + exchange * 2
        + [
            pltpu.VMEM((TOK, HALF), BF16),
            pltpu.VMEM((TOK, D // 16), jnp.int32),
            pltpu.VMEM((TOK, 128), jnp.int32),
            pltpu.VMEM((TOK, CH), F32),
            pltpu.VMEM((D // NS, HALF), BF16),
            pltpu.VMEM((D // NS, HALF), BF16),
            pltpu.VMEM((TOK, HALF), F32),
            pltpu.VMEM((3, CH), F32),
            pltpu.VMEM((256, 2048), BF16),
            pltpu.VMEM((2, 1 + NS, 16, 128), BF16),
            pltpu.VMEM((256, 1024), BF16),
            dma((128,)), dma((128,)), dma((4,)), dma((4,)), dma((8,)), regular, regular,
        ]
        + [dma] * 8,
        compiler_params=pltpu.CompilerParams(
            collective_id=0, has_side_effects=True, vmem_limit_bytes=56 << 20
        ),
    )(
        tokens, sign_in, sign_out, w_value, w_noise, w_gate, conv_taps, conv_taps,
        long_filter,
    )
    return jnp.dot(gated, w_out, preferred_element_type=F32).astype(BF16)


def solution(mesh):
    placed = (
        P(("dp", "seq"), None),
        P(("dp", "seq"), None),
        P(("dp", "seq"), None),
        P("seq", None),
        P("seq", None),
        P(),
        P(),
        P("seq", None),
        P(),
    )
    return jax.shard_map(
        on_device, mesh=mesh, in_specs=placed, out_specs=P(("dp", "seq"), None), check_vma=False
    )
```

```python
import functools

import jax
import jax.numpy as jnp
from jax import lax
from jax.experimental import pallas as pl
from jax.experimental.pallas import tpu as pltpu
from jax.sharding import PartitionSpec as P

MESH = pl.DeviceIdType.MESH
NY, NX, NZ = 4, 4, 8
NS = NY * NX * NZ
SIZE = {"x": NX, "y": NY, "z": NZ}
D, CH, TOK, HALF = 4096, 512, 128, 256
F32, BF16 = jnp.float32, jnp.bfloat16
ROWS = (32, 48, 48)
ORDERS = ("xyz", "zyx", "zxy")


def body(
    tok_ref, sin_ref, sout_ref, wv_ref, wn_ref, wg_ref, taps_ref, gtaps_ref, filt_ref,
    gm_ref,
    wa, wb, wc, tokall, flpall, foall, wg, gpad, halo, fsend, frecv, gcomp, tmat,
    vacc, nacc, stage, vsend, vrecv, xpad, xx, yacc, ysend, yrecv, gmsend,
    sin, sout, fout, wv, wn, filt, gtaps, spread, lagged, shifts,
    ag_send, ag_recv, sib_send, sib_recv, loc_sem, bar_y, bar_z,
    f_send, f_recv, h_send, h_recv, v_send, v_recv, y_send, y_recv,
):
    s = lax.axis_index("seq")
    dp = lax.axis_index("dp")
    pos = {"z": lax.rem(s, NZ), "x": lax.rem(s // NZ, NX), "y": s // (NZ * NX)}

    def at(axis, step):
        p = dict(pos)
        p[axis] = ring(axis, step)
        return {"seq": (p["y"] * NX + p["x"]) * NZ + p["z"], "dp": dp}

    def ring(axis, step):
        return lax.rem(pos[axis] + step + SIZE[axis], SIZE[axis])

    sibling = {"seq": s, "dp": 1 - dp}

    cols = pl.ds(pl.multiple_of(dp * HALF, HALF), HALF)
    cols_other = pl.ds(pl.multiple_of((1 - dp) * HALF, HALF), HALF)
    local = [
        pltpu.make_async_copy(wg_ref.at[:, cols], wg, loc_sem.at[0]),
        pltpu.make_async_copy(tok_ref, tokall.at[pl.ds(0, TOK)], loc_sem.at[1]),
        pltpu.make_async_copy(wv_ref.at[:, cols], wv, loc_sem.at[2]),
        pltpu.make_async_copy(wn_ref.at[:, cols], wn, loc_sem.at[3]),
        pltpu.make_async_copy(filt_ref.at[:, cols], filt, loc_sem.at[4]),
        pltpu.make_async_copy(sin_ref, sin, loc_sem.at[5]),
        pltpu.make_async_copy(gtaps_ref.at[:, pl.ds(CH, CH)], gtaps, loc_sem.at[6]),
    ]
    for i in (2, 3, 4, 1, 5, 0, 6):
        local[i].start()

    bar = pltpu.get_barrier_semaphore()
    for axis in "xyz":
        for step in range(1, SIZE[axis]):
            pl.semaphore_signal(bar, inc=1, device_id=at(axis, step), device_id_type=MESH)
    pl.semaphore_signal(bar, inc=1, device_id=sibling, device_id_type=MESH)

    here = (pos["y"], pos["x"], pos["z"])
    local[2].wait()
    local[3].wait()
    wa[here] = wv[:, :128]
    wb[here] = jnp.concatenate([wn[:, :128], wv[:16, 128:]], axis=0)
    wc[here] = jnp.concatenate([wv[16:, 128:], wn[:, 128:]], axis=0)
    pl.semaphore_wait(bar, 14)

    used = [0]
    sent = []

    def remote(ref, dev):
        i = used[0]
        used[0] += 1
        c = pltpu.make_async_remote_copy(
            src_ref=ref, dst_ref=ref, send_sem=ag_send.at[i], recv_sem=ag_recv.at[i],
            device_id=dev, device_id_type=MESH,
        )
        c.start()
        sent.append(c)
        return c

    def gather(w, order, rows):
        have = []

        def unit(axis, p, half=None):
            idx = {a: (slice(None) if a in have else pos[a]) for a in "yxz"}
            idx[axis] = p
            if half is not None:
                n = SIZE[have[-1]] // 2
                idx[have[-1]] = pl.ds(half * n, n)
            return w.at[idx["y"], idx["x"], idx["z"], rows]

        a = order[0]
        flight = [remote(unit(a, pos[a]), at(a, k)) for k in range(1, SIZE[a])]
        yield
        for c in flight:
            c.wait_recv()
        have.append(a)
        for a in order[1:]:
            for step in range(1, SIZE[a] // 2 + 1):
                last = step == SIZE[a] // 2
                up = remote(unit(a, ring(a, 1 - step), 0 if last else None), at(a, 1))
                down = remote(unit(a, ring(a, step - 1), 1 if last else None), at(a, -1))
                yield
                up.wait_recv()
                down.wait_recv()
            have.append(a)

    def to_all(src, dst, send_sem, recv_sem, first, last):
        def send(i, _):
            peer = lax.rem(s + i, NS)
            pltpu.make_async_remote_copy(
                src_ref=src.at[peer], dst_ref=dst.at[s], send_sem=send_sem, recv_sem=recv_sem,
                device_id={"seq": peer, "dp": dp}, device_id_type=MESH,
            ).start()
            return 0

        lax.fori_loop(first, last, send, 0)

    def all_landed(src, dst, send_sem, recv_sem):
        c = pltpu.make_async_remote_copy(
            src_ref=src.at[pl.ds(0, NS - 1)], dst_ref=dst.at[pl.ds(0, NS - 1)],
            send_sem=send_sem, recv_sem=recv_sem,
            device_id=sibling, device_id_type=MESH,
        )
        c.wait_send()
        c.wait_recv()

    exchange = [
        pltpu.make_async_remote_copy(
            src_ref=src, dst_ref=dst, send_sem=sib_send.at[i], recv_sem=sib_recv.at[i],
            device_id=sibling, device_id_type=MESH,
        )
        for i, (src, dst) in enumerate([
            (tok_ref, tokall.at[pl.ds(TOK, TOK)]),
            (flpall.at[pl.ds(0, TOK)], flpall.at[pl.ds(TOK, TOK)]),
            (fout.at[:, cols_other], foall.at[pl.ds(TOK, TOK)]),
        ])
    ]

    def filter_out():
        exchange[0].start()
        for step in range(1, NY):
            pl.semaphore_signal(bar_y, inc=1, device_id=at("y", step), device_id_type=MESH)
        local[4].wait()
        for c in range(2):
            fsend[:, c, :] = filt[:, pl.ds(128 * c, 128)].T
        pl.semaphore_wait(bar_y, NY - 1)
        for step in range(1, NZ):
            pl.semaphore_signal(bar_z, inc=1, device_id=at("z", step), device_id_type=MESH)

    def send_filter(first, last):
        if first == 1:
            pl.semaphore_wait(bar_z, NZ - 1)
            frecv[s] = fsend[s]
        to_all(fsend, frecv, f_send, f_recv, first, last)

    halo_copy = pltpu.make_async_remote_copy(
        src_ref=gpad.at[:, pl.ds(TOK, 8)], dst_ref=halo, send_sem=h_send, recv_sem=h_recv,
        device_id={"seq": lax.rem(s + 1, NS), "dp": dp}, device_id_type=MESH,
    )

    def gate():
        local[0].wait()
        rows = jnp.dot(tokall[...], wg[...], preferred_element_type=F32).astype(BF16).astype(F32)
        gpad[0, pl.ds(8, TOK)] = rows[:TOK]
        gpad[1, pl.ds(8, TOK)] = rows[TOK:]
        halo_copy.start()

    def bit_table():
        word = lax.broadcasted_iota(jnp.int32, (256, 256), 0)
        place = lax.broadcasted_iota(jnp.int32, (256, 256), 1)
        target = place // 16 + 128 * (lax.rem(place, 16) // 8)
        for i in range(8):
            spread[:, pl.ds(256 * i, 256)] = (word == target + 16 * i).astype(F32).astype(BF16)

    def signs(words, count):
        halves = jnp.concatenate([words & 255, words >> 8], axis=1).astype(F32).astype(BF16)
        found = jnp.dot(halves, spread[:, pl.ds(0, count)], preferred_element_type=F32)
        bit = lax.rem(lax.broadcasted_iota(jnp.int32, (TOK, count), 1), 8)
        return (2 * ((found.astype(jnp.int32) >> bit) & 1) - 1).astype(F32)

    def flip():
        bit_table()
        sout[...] = jnp.zeros_like(sout)
        sout[:, pl.ds(0, 32)] = sout_ref[...]
        for i in (1, 5):
            local[i].wait()
        for i in range(2):
            at_i = pl.ds(2048 * i, 2048)
            turned = signs(sin[:, pl.ds(128 * i, 128)], 2048)
            flpall[pl.ds(0, TOK), at_i] = (tokall[pl.ds(0, TOK), at_i].astype(F32) * turned).astype(BF16)
        fout[...] = signs(sout[...], CH)
        exchange[1].start()
        exchange[2].start()
        foall[pl.ds(0, TOK)] = fout[:, cols]

    lane = lax.broadcasted_iota(jnp.int32, (128, 128), 1)
    row = lax.broadcasted_iota(jnp.int32, (128, 128), 0)

    def compose():
        all_landed(fsend, frecv, f_send, f_recv)
        for c in range(2):
            h = frecv[:, c, :]
            chan = dp * HALF + c * 128 + s
            total = taps_ref[0, chan] * h
            for j in (1, 2):
                turned = pltpu.roll(h, j, 1)
                before = jnp.where(row == 0, 0.0, pltpu.roll(turned, 1, 0))
                total = total + taps_ref[j, chan] * jnp.where(lane < j, before, turned)
            gcomp[c] = total

    def shift_table():
        source = lax.broadcasted_iota(jnp.int32, (256, 128), 0)
        target = lax.broadcasted_iota(jnp.int32, (256, 128), 1) + 128
        for r in range(8):
            shifts[:, pl.ds(128 * r, 128)] = (source == target - 16 * r).astype(F32).astype(BF16)
        lagged[:, 0] = jnp.zeros((2, 16, 128), BF16)

    low_lane = lax.broadcasted_iota(jnp.int32, (16, 128), 1)
    low_row = lax.broadcasted_iota(jnp.int32, (16, 128), 0)

    def toeplitz(c):
        def lags(i, past):
            for k in range(8):
                line = jnp.broadcast_to(gcomp[c, pl.ds(8 * i + k, 1), :], (16, 128))
                turned = pltpu.roll(line, 0, 1, stride=1, stride_axis=0)
                lagged[c, 1 + 8 * i + k] = jnp.where(low_lane >= low_row, turned, past).astype(BF16)
                past = turned
            return past

        lax.fori_loop(0, NS // 8, lags, jnp.zeros((16, 128), F32))

        def expand(i, _):
            k = pl.multiple_of(16 * i, 16)
            pair = jnp.concatenate(
                [
                    lagged[c, pl.ds(k, 16)].reshape(256, 128),
                    lagged[c, pl.ds(k + 1, 16)].reshape(256, 128),
                ],
                axis=1,
            )
            for r in range(0, 8, 2):
                out = jnp.dot(pair, shifts[:, pl.ds(128 * r, 256)], preferred_element_type=F32)
                out = out.astype(BF16)
                tmat[c, pl.ds(k, 16), r] = out[:, :128].reshape(16, 16, 128)
                tmat[c, pl.ds(k, 16), r + 1] = out[:, 128:].reshape(16, 16, 128)
            return 0

        lax.fori_loop(0, NS // 16, expand, 0)

    tasks = [
        filter_out,
        flip,
        lambda: send_filter(1, 64),
        lambda: send_filter(64, NS),
        shift_table,
        compose,
        lambda: toeplitz(0),
    ]
    cuts = (
        ((wa, 0, 16), (wb, 0, 32), (wc, 0, 16)),
        ((wa, 16, 16), (wb, 32, 16), (wc, 16, 32)),
    )
    running = [
        [gather(w, order, pl.ds(first, rows)) for (w, first, rows), order in zip(cut, ORDERS)]
        for cut in cuts
    ]
    while running:
        for group in list(running):
            for g in list(group):
                try:
                    next(g)
                except StopIteration:
                    group.remove(g)
            if not group:
                running.remove(group)
            if tasks and (len(tasks) < 7 or group is running[-1]):
                tasks.pop(0)()
    for task in tasks:
        task()

    for c in exchange:
        c.wait()
    def project(y, _):
        k = pl.ds(pl.multiple_of(y * 1024, 1024), 1024)
        pa, pb, pc = (w[y].reshape(32, r, 128) for w, r in zip((wa, wb, wc), ROWS))
        right = jnp.concatenate([pb[:, 32:], pc[:, :16]], axis=1).reshape(1024, 128)
        value = jnp.concatenate([pa.reshape(1024, 128), right], axis=1)
        noise = jnp.concatenate(
            [pb[:, :32].reshape(1024, 128), pc[:, 16:].reshape(1024, 128)], axis=1
        )
        more_v = jnp.dot(tokall[:, k], value, preferred_element_type=F32)
        more_n = jnp.dot(flpall[:, k], noise, preferred_element_type=F32)
        vacc[...] += more_v
        nacc[...] += more_n
        return 0

    vacc[...] = jnp.zeros_like(vacc)
    nacc[...] = jnp.zeros_like(nacc)
    lax.fori_loop(0, NY, project, 0)
    value_rows = (vacc[...] + foall[...] * nacc[...]).astype(BF16).astype(F32)
    for p in range(2):
        for c in range(2):
            stage[:, 2 * p + c, :] = value_rows[128 * p : 128 * p + 128, 128 * c : 128 * c + 128].T
    vsend[...] = stage[...].astype(BF16)
    vrecv[s] = vsend[s]
    to_all(vsend, vrecv, v_send, v_recv, 1, NS)
    gate()
    toeplitz(1)
    all_landed(vsend, vrecv, v_send, v_recv)

    stage[...] = vrecv[...].astype(F32)
    xpad[:, pl.ds(0, 16), :] = jnp.zeros((4, 16, 128), F32)
    for p in range(2):
        for c in range(2):
            xpad[2 * p + c, pl.ds(16, 128), :] = stage[:, 2 * p + c, :]
    for p in range(2):
        for c in range(2):
            for r in range(16):
                late = xpad[2 * p + c, pl.ds(16 - r, 128), :].astype(BF16)
                xx[c, r // 2, :, p, :, pl.ds(128 * (r % 2), 128)] = late.reshape(8, 16, 128)
    for c in range(2):
        for u in range(8):
            m = 8 - u
            total = None
            for k in range(8):
                part = jnp.dot(
                    xx[c, k, pl.ds(0, m)].reshape(32 * m, 256),
                    tmat[c, pl.ds(2 * (8 * u + k), 2)].reshape(256, 128),
                    preferred_element_type=F32,
                )
                total = part if total is None else total + part
            total = total.reshape(m, 2, 16, 128)
            if u == 0:
                yacc[c] = total
            else:
                yacc[c, pl.ds(u, m)] += total
        for p in range(2):
            stage[:, 2 * p + c, :] = yacc[c, :, p].reshape(128, 128)
    ysend[...] = stage[...].astype(BF16)
    yrecv[s] = ysend[s]
    to_all(ysend, yrecv, y_send, y_recv, 1, NS)
    for c in sent:
        c.wait_send()

    halo_copy.wait()
    for p in range(2):
        gpad[p, pl.ds(0, 8)] = jnp.where(s == 0, 0.0, halo[p])
    all_landed(ysend, yrecv, y_send, y_recv)
    stage[...] = yrecv[...].astype(F32)
    local[6].wait()
    taps = gtaps[:, cols]

    def mixed(p):
        short = taps[0:1] * gpad[p, pl.ds(8, TOK)]
        for j in (1, 2):
            short = short + taps[j : j + 1] * gpad[p, pl.ds(8 - j, TOK)]
        mix = jnp.concatenate([stage[:, 2 * p + c, :].T for c in range(2)], axis=1)
        return (short * mix).astype(BF16)

    gmsend[...] = mixed(1)
    swap = pltpu.make_async_remote_copy(
        src_ref=gmsend, dst_ref=gm_ref.at[:, cols], send_sem=sib_send.at[3],
        recv_sem=sib_recv.at[3], device_id=sibling, device_id_type=MESH,
    )
    swap.start()
    gm_ref[:, cols] = mixed(0)
    swap.wait()


def on_device(tokens, sign_in, sign_out, w_value, w_noise, w_gate, conv_taps, long_filter, w_out):
    vmem = pl.BlockSpec(memory_space=pltpu.VMEM)
    hbm = pl.BlockSpec(memory_space=pl.ANY)
    dma, regular = pltpu.SemaphoreType.DMA, pltpu.SemaphoreType.REGULAR
    exchange = [pltpu.VMEM((NS, 4, 128), BF16)]
    gated = pl.pallas_call(
        body,
        out_shape=jax.ShapeDtypeStruct((TOK, CH), BF16),
        in_specs=[
            hbm, hbm, vmem, hbm, hbm, hbm, pl.BlockSpec(memory_space=pltpu.SMEM), hbm, hbm,
        ],
        out_specs=vmem,
        scratch_shapes=[pltpu.VMEM((NY, NX, NZ, r, 128), BF16) for r in ROWS]
        + [
            pltpu.VMEM((2 * TOK, D), BF16),
            pltpu.VMEM((2 * TOK, D), BF16),
            pltpu.VMEM((2 * TOK, HALF), F32),
            pltpu.VMEM((D, HALF), BF16),
            pltpu.VMEM((2, 8 + TOK, HALF), F32),
            pltpu.VMEM((2, 8, HALF), F32),
            pltpu.VMEM((NS, 2, 128), F32),
            pltpu.VMEM((NS, 2, 128), F32),
            pltpu.VMEM((2, 128, 128), F32),
            pltpu.VMEM((2, NS, 8, 16, 128), BF16),
            pltpu.VMEM((2 * TOK, HALF), F32),
            pltpu.VMEM((2 * TOK, HALF), F32),
            pltpu.VMEM((NS, 4, 128), F32),
        ]
        + exchange * 2
        + [
            pltpu.VMEM((4, 16 + TOK, 128), F32),
            pltpu.VMEM((2, 8, 8, 2, 16, 256), BF16),
            pltpu.VMEM((2, 8, 2, 16, 128), F32),
        ]
        + exchange * 2
        + [
            pltpu.VMEM((TOK, HALF), BF16),
            pltpu.VMEM((TOK, D // 16), jnp.int32),
            pltpu.VMEM((TOK, 128), jnp.int32),
            pltpu.VMEM((TOK, CH), F32),
            pltpu.VMEM((D // NS, HALF), BF16),
            pltpu.VMEM((D // NS, HALF), BF16),
            pltpu.VMEM((TOK, HALF), F32),
            pltpu.VMEM((3, CH), F32),
            pltpu.VMEM((256, 2048), BF16),
            pltpu.VMEM((2, 1 + NS, 16, 128), BF16),
            pltpu.VMEM((256, 1024), BF16),
            dma((160,)), dma((160,)), dma((4,)), dma((4,)), dma((8,)), regular, regular,
        ]
        + [dma] * 8,
        compiler_params=pltpu.CompilerParams(
            collective_id=0, has_side_effects=True, vmem_limit_bytes=40 << 20
        ),
    )(
        *[pltpu.with_memory_space_constraint(x, pltpu.HBM) for x in (tokens, sign_in)], sign_out,
        *[pltpu.with_memory_space_constraint(x, pltpu.HBM) for x in (w_value, w_noise, w_gate)], conv_taps,
        *[pltpu.with_memory_space_constraint(x, pltpu.HBM) for x in (conv_taps, long_filter)],
    )
    return jnp.dot(gated, w_out, preferred_element_type=F32).astype(BF16)


def solution(mesh):
    placed = (
        P(("dp", "seq"), None),
        P(("dp", "seq"), None),
        P(("dp", "seq"), None),
        P("seq", None),
        P("seq", None),
        P(),
        P(),
        P("seq", None),
        P(),
    )
    return jax.shard_map(
        on_device, mesh=mesh, in_specs=placed, out_specs=P(("dp", "seq"), None), check_vma=False
    )
```

```python
import functools

import jax
import jax.numpy as jnp
from jax import lax
from jax.experimental import pallas as pl
from jax.experimental.pallas import tpu as pltpu
from jax.sharding import PartitionSpec as P

MESH = pl.DeviceIdType.MESH
NY, NX, NZ = 4, 4, 8
NS = NY * NX * NZ
SIZE = {"x": NX, "y": NY, "z": NZ}
D, CH, TOK, HALF = 4096, 512, 128, 256
F32, BF16 = jnp.float32, jnp.bfloat16
ROWS = (32, 48, 48)
ORDERS = ("xyz", "zyx", "zxy")


def body(
    tok_ref, sin_ref, sout_ref, wv_ref, wn_ref, wg_ref, taps_ref, gtaps_ref, filt_ref,
    gm_ref,
    wa, wb, wc, tokall, flpall, foall, wg, gpad, halo, fsend, frecv, gcomp, tmat,
    vacc, nacc, stage, vsend, vrecv, xpad, xx, yacc, ysend, yrecv, gmsend,
    sin, sout, fout, wv, wn, filt, gtaps, spread, lagged, shifts,
    ag_send, ag_recv, sib_send, sib_recv, loc_sem, bar_y, bar_z,
    f_send, f_recv, h_send, h_recv, v_send, v_recv, y_send, y_recv,
):
    s = lax.axis_index("seq")
    dp = lax.axis_index("dp")
    pos = {"z": lax.rem(s, NZ), "x": lax.rem(s // NZ, NX), "y": s // (NZ * NX)}

    def at(axis, step):
        p = dict(pos)
        p[axis] = ring(axis, step)
        return {"seq": (p["y"] * NX + p["x"]) * NZ + p["z"], "dp": dp}

    def ring(axis, step):
        return lax.rem(pos[axis] + step + SIZE[axis], SIZE[axis])

    sibling = {"seq": s, "dp": 1 - dp}

    cols = pl.ds(pl.multiple_of(dp * HALF, HALF), HALF)
    cols_other = pl.ds(pl.multiple_of((1 - dp) * HALF, HALF), HALF)
    local = [
        pltpu.make_async_copy(wg_ref.at[:, cols], wg, loc_sem.at[0]),
        pltpu.make_async_copy(tok_ref, tokall.at[pl.ds(0, TOK)], loc_sem.at[1]),
        pltpu.make_async_copy(wv_ref.at[:, cols], wv, loc_sem.at[2]),
        pltpu.make_async_copy(wn_ref.at[:, cols], wn, loc_sem.at[3]),
        pltpu.make_async_copy(filt_ref.at[:, cols], filt, loc_sem.at[4]),
        pltpu.make_async_copy(sin_ref, sin, loc_sem.at[5]),
        pltpu.make_async_copy(gtaps_ref.at[:, pl.ds(CH, CH)], gtaps, loc_sem.at[6]),
    ]
    for i in (2, 3, 4, 1, 5, 0, 6):
        local[i].start()

    bar = pltpu.get_barrier_semaphore()
    for axis in "xyz":
        for step in range(1, SIZE[axis]):
            pl.semaphore_signal(bar, inc=1, device_id=at(axis, step), device_id_type=MESH)
    pl.semaphore_signal(bar, inc=1, device_id=sibling, device_id_type=MESH)

    here = (pos["y"], pos["x"], pos["z"])
    local[2].wait()
    local[3].wait()
    wa[here] = wv[:, :128]
    wb[here] = jnp.concatenate([wn[:, :128], wv[:16, 128:]], axis=0)
    wc[here] = jnp.concatenate([wv[16:, 128:], wn[:, 128:]], axis=0)
    pl.semaphore_wait(bar, 14)

    used = [0]
    sent = []

    def remote(ref, dev):
        i = used[0]
        used[0] += 1
        c = pltpu.make_async_remote_copy(
            src_ref=ref, dst_ref=ref, send_sem=ag_send.at[i], recv_sem=ag_recv.at[i],
            device_id=dev, device_id_type=MESH,
        )
        c.start()
        sent.append(c)
        return c

    def gather(w, order, rows):
        have = []

        def unit(axis, p, half=None):
            idx = {a: (slice(None) if a in have else pos[a]) for a in "yxz"}
            idx[axis] = p
            if half is not None:
                n = SIZE[have[-1]] // 2
                idx[have[-1]] = pl.ds(half * n, n)
            return w.at[idx["y"], idx["x"], idx["z"], rows]

        a = order[0]
        flight = [remote(unit(a, pos[a]), at(a, k)) for k in range(1, SIZE[a])]
        yield
        for c in flight:
            c.wait_recv()
        have.append(a)
        for a in order[1:]:
            for step in range(1, SIZE[a] // 2 + 1):
                last = step == SIZE[a] // 2
                up = remote(unit(a, ring(a, 1 - step), 0 if last else None), at(a, 1))
                down = remote(unit(a, ring(a, step - 1), 1 if last else None), at(a, -1))
                yield
                up.wait_recv()
                down.wait_recv()
            have.append(a)

    def to_all(src, dst, send_sem, recv_sem, first, last):
        def send(i, _):
            peer = lax.rem(s + i, NS)
            pltpu.make_async_remote_copy(
                src_ref=src.at[peer], dst_ref=dst.at[s], send_sem=send_sem, recv_sem=recv_sem,
                device_id={"seq": peer, "dp": dp}, device_id_type=MESH,
            ).start()
            return 0

        lax.fori_loop(first, last, send, 0)

    def all_landed(src, dst, send_sem, recv_sem):
        c = pltpu.make_async_remote_copy(
            src_ref=src.at[pl.ds(0, NS - 1)], dst_ref=dst.at[pl.ds(0, NS - 1)],
            send_sem=send_sem, recv_sem=recv_sem,
            device_id=sibling, device_id_type=MESH,
        )
        c.wait_send()
        c.wait_recv()

    exchange = [
        pltpu.make_async_remote_copy(
            src_ref=src, dst_ref=dst, send_sem=sib_send.at[i], recv_sem=sib_recv.at[i],
            device_id=sibling, device_id_type=MESH,
        )
        for i, (src, dst) in enumerate([
            (tok_ref, tokall.at[pl.ds(TOK, TOK)]),
            (flpall.at[pl.ds(0, TOK)], flpall.at[pl.ds(TOK, TOK)]),
            (fout.at[:, cols_other], foall.at[pl.ds(TOK, TOK)]),
        ])
    ]

    def filter_out():
        exchange[0].start()
        for step in range(1, NY):
            pl.semaphore_signal(bar_y, inc=1, device_id=at("y", step), device_id_type=MESH)
        local[4].wait()
        for c in range(2):
            fsend[:, c, :] = filt[:, pl.ds(128 * c, 128)].T
        pl.semaphore_wait(bar_y, NY - 1)
        for step in range(1, NZ):
            pl.semaphore_signal(bar_z, inc=1, device_id=at("z", step), device_id_type=MESH)

    def send_filter(first, last):
        if first == 1:
            pl.semaphore_wait(bar_z, NZ - 1)
            frecv[s] = fsend[s]
        to_all(fsend, frecv, f_send, f_recv, first, last)

    halo_copy = pltpu.make_async_remote_copy(
        src_ref=gpad.at[:, pl.ds(TOK, 8)], dst_ref=halo, send_sem=h_send, recv_sem=h_recv,
        device_id={"seq": lax.rem(s + 1, NS), "dp": dp}, device_id_type=MESH,
    )

    def gate():
        local[0].wait()
        rows = jnp.dot(tokall[...], wg[...], preferred_element_type=F32).astype(BF16).astype(F32)
        gpad[0, pl.ds(8, TOK)] = rows[:TOK]
        gpad[1, pl.ds(8, TOK)] = rows[TOK:]
        halo_copy.start()

    def bit_table():
        word = lax.broadcasted_iota(jnp.int32, (256, 256), 0)
        place = lax.broadcasted_iota(jnp.int32, (256, 256), 1)
        target = place // 16 + 128 * (lax.rem(place, 16) // 8)
        for i in range(8):
            spread[:, pl.ds(256 * i, 256)] = (word == target + 16 * i).astype(F32).astype(BF16)

    def signs(words, count):
        halves = jnp.concatenate([words & 255, words >> 8], axis=1).astype(F32).astype(BF16)
        found = jnp.dot(halves, spread[:, pl.ds(0, count)], preferred_element_type=F32)
        bit = lax.rem(lax.broadcasted_iota(jnp.int32, (TOK, count), 1), 8)
        return (2 * ((found.astype(jnp.int32) >> bit) & 1) - 1).astype(F32)

    def flip():
        bit_table()
        sout[...] = jnp.zeros_like(sout)
        sout[:, pl.ds(0, 32)] = sout_ref[...]
        for i in (1, 5):
            local[i].wait()
        for i in range(2):
            at_i = pl.ds(2048 * i, 2048)
            turned = signs(sin[:, pl.ds(128 * i, 128)], 2048)
            flpall[pl.ds(0, TOK), at_i] = (tokall[pl.ds(0, TOK), at_i].astype(F32) * turned).astype(BF16)
        fout[...] = signs(sout[...], CH)
        exchange[1].start()
        exchange[2].start()
        foall[pl.ds(0, TOK)] = fout[:, cols]

    lane = lax.broadcasted_iota(jnp.int32, (128, 128), 1)
    row = lax.broadcasted_iota(jnp.int32, (128, 128), 0)

    def compose():
        all_landed(fsend, frecv, f_send, f_recv)
        for c in range(2):
            h = frecv[:, c, :]
            chan = dp * HALF + c * 128 + s
            total = taps_ref[0, chan] * h
            for j in (1, 2):
                turned = pltpu.roll(h, j, 1)
                before = jnp.where(row == 0, 0.0, pltpu.roll(turned, 1, 0))
                total = total + taps_ref[j, chan] * jnp.where(lane < j, before, turned)
            gcomp[c] = total

    def shift_table():
        source = lax.broadcasted_iota(jnp.int32, (256, 128), 0)
        target = lax.broadcasted_iota(jnp.int32, (256, 128), 1) + 128
        for r in range(8):
            shifts[:, pl.ds(128 * r, 128)] = (source == target - 16 * r).astype(F32).astype(BF16)
        lagged[:, 0] = jnp.zeros((2, 16, 128), BF16)

    low_lane = lax.broadcasted_iota(jnp.int32, (16, 128), 1)
    low_row = lax.broadcasted_iota(jnp.int32, (16, 128), 0)

    def toeplitz(c):
        def lags(i, past):
            for k in range(8):
                line = jnp.broadcast_to(gcomp[c, pl.ds(8 * i + k, 1), :], (16, 128))
                turned = pltpu.roll(line, 0, 1, stride=1, stride_axis=0)
                lagged[c, 1 + 8 * i + k] = jnp.where(low_lane >= low_row, turned, past).astype(BF16)
                past = turned
            return past

        lax.fori_loop(0, NS // 8, lags, jnp.zeros((16, 128), F32))

        def expand(i, _):
            k = pl.multiple_of(16 * i, 16)
            pair = jnp.concatenate(
                [
                    lagged[c, pl.ds(k, 16)].reshape(256, 128),
                    lagged[c, pl.ds(k + 1, 16)].reshape(256, 128),
                ],
                axis=1,
            )
            for r in range(0, 8, 2):
                out = jnp.dot(pair, shifts[:, pl.ds(128 * r, 256)], preferred_element_type=F32)
                out = out.astype(BF16)
                tmat[c, pl.ds(k, 16), r] = out[:, :128].reshape(16, 16, 128)
                tmat[c, pl.ds(k, 16), r + 1] = out[:, 128:].reshape(16, 16, 128)
            return 0

        lax.fori_loop(0, NS // 16, expand, 0)

    tasks = [
        filter_out,
        flip,
        lambda: send_filter(1, 64),
        lambda: send_filter(64, NS),
        shift_table,
        compose,
        lambda: toeplitz(0),
    ]
    cuts = (
        ((wa, 0, 16), (wb, 0, 32), (wc, 0, 16)),
        ((wa, 16, 16), (wb, 32, 16), (wc, 16, 32)),
    )
    running = [
        [gather(w, order, pl.ds(first, rows)) for (w, first, rows), order in zip(cut, ORDERS)]
        for cut in cuts
    ]

    def advance(group, g):
        try:
            next(g)
        except StopIteration:
            group.remove(g)

    along_z = [group[0] for group in running]
    turns = 0
    while running:
        turns += 1
        for group in list(running):
            for g in list(group):
                advance(group, g)
            if not group:
                running.remove(group)
            if tasks and (len(tasks) < 7 or group is running[-1]):
                tasks.pop(0)()
        if turns >= 4:
            for group in running:
                for g in list(group):
                    if g in along_z:
                        advance(group, g)
    for task in tasks:
        task()

    for c in exchange:
        c.wait()
    def project(y, _):
        k = pl.ds(pl.multiple_of(y * 1024, 1024), 1024)
        pa, pb, pc = (w[y].reshape(32, r, 128) for w, r in zip((wa, wb, wc), ROWS))
        right = jnp.concatenate([pb[:, 32:], pc[:, :16]], axis=1).reshape(1024, 128)
        value = jnp.concatenate([pa.reshape(1024, 128), right], axis=1)
        noise = jnp.concatenate(
            [pb[:, :32].reshape(1024, 128), pc[:, 16:].reshape(1024, 128)], axis=1
        )
        more_v = jnp.dot(tokall[:, k], value, preferred_element_type=F32)
        more_n = jnp.dot(flpall[:, k], noise, preferred_element_type=F32)
        vacc[...] += more_v
        nacc[...] += more_n
        return 0

    vacc[...] = jnp.zeros_like(vacc)
    nacc[...] = jnp.zeros_like(nacc)
    lax.fori_loop(0, NY, project, 0)
    value_rows = (vacc[...] + foall[...] * nacc[...]).astype(BF16).astype(F32)
    for p in range(2):
        for c in range(2):
            stage[:, 2 * p + c, :] = value_rows[128 * p : 128 * p + 128, 128 * c : 128 * c + 128].T
    vsend[...] = stage[...].astype(BF16)
    vrecv[s] = vsend[s]
    to_all(vsend, vrecv, v_send, v_recv, 1, NS)
    gate()
    toeplitz(1)
    all_landed(vsend, vrecv, v_send, v_recv)

    stage[...] = vrecv[...].astype(F32)
    xpad[:, pl.ds(0, 16), :] = jnp.zeros((4, 16, 128), F32)
    for p in range(2):
        for c in range(2):
            xpad[2 * p + c, pl.ds(16, 128), :] = stage[:, 2 * p + c, :]
    for p in range(2):
        for c in range(2):
            for r in range(16):
                late = xpad[2 * p + c, pl.ds(16 - r, 128), :].astype(BF16)
                xx[c, r // 2, :, p, :, pl.ds(128 * (r % 2), 128)] = late.reshape(8, 16, 128)
    for c in range(2):
        for u in range(8):
            m = 8 - u
            total = None
            for k in range(8):
                part = jnp.dot(
                    xx[c, k, pl.ds(0, m)].reshape(32 * m, 256),
                    tmat[c, pl.ds(2 * (8 * u + k), 2)].reshape(256, 128),
                    preferred_element_type=F32,
                )
                total = part if total is None else total + part
            total = total.reshape(m, 2, 16, 128)
            if u == 0:
                yacc[c] = total
            else:
                yacc[c, pl.ds(u, m)] += total
        for p in range(2):
            stage[:, 2 * p + c, :] = yacc[c, :, p].reshape(128, 128)
    ysend[...] = stage[...].astype(BF16)
    yrecv[s] = ysend[s]
    to_all(ysend, yrecv, y_send, y_recv, 1, NS)
    for c in sent:
        c.wait_send()

    halo_copy.wait()
    for p in range(2):
        gpad[p, pl.ds(0, 8)] = jnp.where(s == 0, 0.0, halo[p])
    all_landed(ysend, yrecv, y_send, y_recv)
    stage[...] = yrecv[...].astype(F32)
    local[6].wait()
    taps = gtaps[:, cols]

    def mixed(p):
        short = taps[0:1] * gpad[p, pl.ds(8, TOK)]
        for j in (1, 2):
            short = short + taps[j : j + 1] * gpad[p, pl.ds(8 - j, TOK)]
        mix = jnp.concatenate([stage[:, 2 * p + c, :].T for c in range(2)], axis=1)
        return (short * mix).astype(BF16)

    gmsend[...] = mixed(1)
    swap = pltpu.make_async_remote_copy(
        src_ref=gmsend, dst_ref=gm_ref.at[:, cols], send_sem=sib_send.at[3],
        recv_sem=sib_recv.at[3], device_id=sibling, device_id_type=MESH,
    )
    swap.start()
    gm_ref[:, cols] = mixed(0)
    swap.wait()


def on_device(tokens, sign_in, sign_out, w_value, w_noise, w_gate, conv_taps, long_filter, w_out):
    vmem = pl.BlockSpec(memory_space=pltpu.VMEM)
    hbm = pl.BlockSpec(memory_space=pl.ANY)
    dma, regular = pltpu.SemaphoreType.DMA, pltpu.SemaphoreType.REGULAR
    exchange = [pltpu.VMEM((NS, 4, 128), BF16)]
    gated = pl.pallas_call(
        body,
        out_shape=jax.ShapeDtypeStruct((TOK, CH), BF16),
        in_specs=[
            hbm, hbm, vmem, hbm, hbm, hbm, pl.BlockSpec(memory_space=pltpu.SMEM), hbm, hbm,
        ],
        out_specs=vmem,
        scratch_shapes=[pltpu.VMEM((NY, NX, NZ, r, 128), BF16) for r in ROWS]
        + [
            pltpu.VMEM((2 * TOK, D), BF16),
            pltpu.VMEM((2 * TOK, D), BF16),
            pltpu.VMEM((2 * TOK, HALF), F32),
            pltpu.VMEM((D, HALF), BF16),
            pltpu.VMEM((2, 8 + TOK, HALF), F32),
            pltpu.VMEM((2, 8, HALF), F32),
            pltpu.VMEM((NS, 2, 128), F32),
            pltpu.VMEM((NS, 2, 128), F32),
            pltpu.VMEM((2, 128, 128), F32),
            pltpu.VMEM((2, NS, 8, 16, 128), BF16),
            pltpu.VMEM((2 * TOK, HALF), F32),
            pltpu.VMEM((2 * TOK, HALF), F32),
            pltpu.VMEM((NS, 4, 128), F32),
        ]
        + exchange * 2
        + [
            pltpu.VMEM((4, 16 + TOK, 128), F32),
            pltpu.VMEM((2, 8, 8, 2, 16, 256), BF16),
            pltpu.VMEM((2, 8, 2, 16, 128), F32),
        ]
        + exchange * 2
        + [
            pltpu.VMEM((TOK, HALF), BF16),
            pltpu.VMEM((TOK, D // 16), jnp.int32),
            pltpu.VMEM((TOK, 128), jnp.int32),
            pltpu.VMEM((TOK, CH), F32),
            pltpu.VMEM((D // NS, HALF), BF16),
            pltpu.VMEM((D // NS, HALF), BF16),
            pltpu.VMEM((TOK, HALF), F32),
            pltpu.VMEM((3, CH), F32),
            pltpu.VMEM((256, 2048), BF16),
            pltpu.VMEM((2, 1 + NS, 16, 128), BF16),
            pltpu.VMEM((256, 1024), BF16),
            dma((160,)), dma((160,)), dma((4,)), dma((4,)), dma((8,)), regular, regular,
        ]
        + [dma] * 8,
        compiler_params=pltpu.CompilerParams(
            collective_id=0, has_side_effects=True, vmem_limit_bytes=40 << 20
        ),
    )(
        *[pltpu.with_memory_space_constraint(x, pltpu.HBM) for x in (tokens, sign_in)], sign_out,
        *[pltpu.with_memory_space_constraint(x, pltpu.HBM) for x in (w_value, w_noise, w_gate)], conv_taps,
        *[pltpu.with_memory_space_constraint(x, pltpu.HBM) for x in (conv_taps, long_filter)],
    )
    return jnp.dot(gated, w_out, preferred_element_type=F32).astype(BF16)


def solution(mesh):
    placed = (
        P(("dp", "seq"), None),
        P(("dp", "seq"), None),
        P(("dp", "seq"), None),
        P("seq", None),
        P("seq", None),
        P(),
        P(),
        P("seq", None),
        P(),
    )
    return jax.shard_map(
        on_device, mesh=mesh, in_specs=placed, out_specs=P(("dp", "seq"), None), check_vma=False
    )
```
